32 devices in a mesh: row: 4 (over z), col: 8 (over y, x, core).
Axes of the slice: x: 2, y: 2, z: 4, core: 2. Of those that a mesh axis runs over, the one named last changes fastest.
Arguments:
- train_rows: bfloat16 [2048, 1024], P(('row', 'col')), may hold values from -6 to 6
- eval_rows: bfloat16 [4096, 1024], P(('col', 'row')), may hold values from -6 to 6
- tile_mask: int32 [4, 8], P('row', 'col'), may hold values from 0 to 1, as said below
Outputs:
- best_match: float32 [2048], P(('row', 'col'))
- near_count: float32 [2048], P(('row', 'col'))
The draws below stay inside these ranges and needn't reach their ends.
Inputs may be any that keep to these rules, and one draw needn't show every extreme that they name: `tile_mask`: 1 keeps a tile; every tile row keeps at least one tile; rows and columns of tiles keep very different numbers of tiles.
All inputs are finite; a program needn't handle non-finite values.
Results may differ from the reference program's by a relative error of at most 0.0003.
Values may be sent and summed in bfloat16 or wider, within the bound.
No kernel may reach another device: no remote copies, remote signals or barrier semaphores. Data moves between devices by JAX's collectives and lax.ppermute only.
A program may use at most 64 MiB of HBM per device.

```python
import jax
import jax.numpy as jnp
from jax import lax

D = 1024
TILE = 512
NA = 2048
NB = 4096
NTA = 4
NTB = 8
TILES_A = 1
TILES_B = 1


clusters = 16


def member_table(key, count, group):
    first, second = jax.random.split(key)
    richness = jax.random.randint(first, (count // group,), 1, 5)
    richness = jnp.repeat(richness, group)
    draws = jax.random.randint(second, (count, clusters), 0, 64)
    return (draws < 4 * richness[:, None]).astype(jnp.int32)


def draw_tile_mask(key, part):
    key_rows = jax.random.fold_in(key, 11)
    key_cols = jax.random.fold_in(key, 23)
    rows_member = member_table(key_rows, NTA, TILES_A)
    cols_member = member_table(key_cols, NTB, TILES_B)
    shared = jnp.dot(rows_member, cols_member.T)
    forced_col = (jnp.arange(NTA, dtype=jnp.int32) * 5 + 3) % NTB
    forced = jnp.arange(NTB, dtype=jnp.int32)[None, :] == forced_col[:, None]
    return jnp.logical_or(shared > 0, forced).astype(jnp.int32)


def shard_levels(stream_key, dims, cuts, smallest, top_value):
    factor_of, own = 1.0, jax.random.fold_in(stream_key, 6)
    for dim, shards_of in cuts:
        steps = jnp.exp(jax.random.uniform(jax.random.fold_in(own, dim), (shards_of,), jnp.float32, smallest / len(cuts), top_value / len(cuts)))
        factor_of = factor_of * jnp.repeat(steps, dims[dim] // shards_of).reshape([-1 if axis == dim else 1 for axis in range(len(dims))])
    return factor_of


def gaussian(own_key, shape, deviation, bound, cuts=(), kind=jnp.bfloat16):
    result = jax.random.normal(own_key, shape, jnp.float32) * deviation
    if len(cuts) > 0:
        result = shard_levels(own_key, shape, cuts, -0.22, 0.18) * result
    return jnp.clip(result, min=-bound, max=bound).astype(kind)


def setup_inputs(seed: int = 0) -> dict:
    key_of = jax.random.split(jax.random.key(seed), 4)
    train_rows = gaussian(key_of[0], (NA, D), 1.0, 6.0, ((0, 32),))
    eval_rows = gaussian(key_of[1], (NB, D), 1.0, 6.0, ((0, 32),))
    tile_mask = draw_tile_mask(jax.random.fold_in(key_of[3], 71), 0)
    return dict(train_rows=train_rows, eval_rows=eval_rows, tile_mask=tile_mask)


threshold = 2.5
sharpness = 4.0
floor_value = -1e30


def reference(train_rows, eval_rows, tile_mask):
    factor = D ** -0.5
    left = train_rows.astype(jnp.float32).reshape(NTA, TILE, D)
    right = eval_rows.astype(jnp.float32).reshape(NTB, TILE, D)

    def one_block(inputs):
        block, mask_row = inputs

        def advance(carry, pair):
            tile, flag = pair

            def compute(state):
                scores = jnp.dot(block, tile.T, precision=lax.Precision.HIGHEST) * factor
                soft = jax.nn.sigmoid(sharpness * (scores - threshold))
                return (jnp.maximum(state[0], jnp.max(scores, axis=1)), state[1] + jnp.sum(soft, axis=1))

            def unchanged(state):
                return state

            return lax.cond(flag > 0, compute, unchanged, carry), None

        initial = (jnp.full((TILE,), floor_value, jnp.float32), jnp.zeros((TILE,), jnp.float32))
        (maxima, counts), _ = lax.scan(advance, initial, (right, mask_row))
        return maxima, jnp.log1p(counts)

    maxima, near = lax.map(one_block, (left, tile_mask))
    return maxima.reshape(NA), near.reshape(NA)
```

```python
import functools

import jax
import jax.numpy as jnp
from jax import lax
from jax.experimental import pallas as pl
from jax.experimental.pallas import tpu as pltpu
from jax.sharding import PartitionSpec as P

TILE = 512
threshold = 2.5
sharpness = 4.0
floor_value = -1e30


def pair_kernel(n_eval, n_train, factor, *refs):
    evals, trains = refs[:n_eval], refs[n_eval : n_eval + n_train]
    out, eval_buf, train_buf, sem_e, sem_t = refs[n_eval + n_train :]
    rows = trains[0].shape[0]
    t_copies = [
        pltpu.make_async_copy(t, train_buf.at[pl.ds(i * rows, rows)], sem_t.at[i])
        for i, t in enumerate(trains)
    ]
    e_copies = [
        pltpu.make_async_copy(e, eval_buf.at[i], sem_e.at[i]) for i, e in enumerate(evals)
    ]
    for copy in t_copies + e_copies:
        copy.start()
    for copy in t_copies:
        copy.wait()
    for j in range(n_eval):
        e_copies[j].wait()
        scores = factor * lax.dot_general(
            eval_buf[j],
            train_buf[...],
            (((1,), (1,)), ((), ())),
            preferred_element_type=jnp.float32,
        )
        soft = jax.nn.sigmoid(sharpness * (scores - threshold))
        out[j, :] = jnp.max(scores, axis=0)
        out[n_eval + j, :] = jnp.sum(soft, axis=0)


def pair_stats(evals, trains):
    n_eval, n_train = len(evals), len(trains)
    (e_rows, d), (t_rows, _) = evals[0].shape, trains[0].shape
    return pl.pallas_call(
        functools.partial(pair_kernel, n_eval, n_train, d**-0.5),
        out_shape=jax.ShapeDtypeStruct((2 * n_eval, n_train * t_rows), jnp.float32),
        in_specs=[pl.BlockSpec(memory_space=pl.ANY)] * (n_eval + n_train),
        out_specs=pl.BlockSpec(memory_space=pltpu.VMEM),
        scratch_shapes=[
            pltpu.VMEM((n_eval, e_rows, d), evals[0].dtype),
            pltpu.VMEM((n_train * t_rows, d), trains[0].dtype),
            pltpu.SemaphoreType.DMA((n_eval,)),
            pltpu.SemaphoreType.DMA((n_train,)),
        ],
        compiler_params=pltpu.CompilerParams(vmem_limit_bytes=32 * 2**20),
    )(*evals, *trains)


def on_device(train_rows, eval_rows, tile_mask):
    rows, cols = lax.axis_size("row"), lax.axis_size("col")
    chips = cols // 2
    swap = [(c, c ^ 1) for c in range(cols)]

    def far(x, d):
        return lax.ppermute(
            x, "col", [((c + 2 * d) % cols, c) for c in range(cols)]
        )

    def along(x, d):
        return lax.ppermute(x, "row", [(r, (r + d) % rows) for r in range(rows)])

    def over_col(x):
        mine = [x] + [far(x, d) for d in range(1, chips)]
        return mine + [lax.ppermute(m, "col", swap) for m in mine]

    evals = over_col(eval_rows)
    trains = [train_rows] + [along(train_rows, d) for d in range(1, rows)]
    masks = jnp.stack(over_col(tile_mask))
    n = len(evals)
    t_rows, e_rows = train_rows.shape[0], eval_rows.shape[0]
    stats = pair_stats(evals, trains)
    parts = [stats[:, i * t_rows : (i + 1) * t_rows] for i in range(rows)]
    back = [parts[0]] + [along(parts[d], rows - d) for d in range(1, rows)]

    row, col = lax.axis_index("row"), lax.axis_index("col")
    kept = lax.dynamic_index_in_dim(masks, col * t_rows // TILE, 1, keepdims=False)
    best, soft = [], []
    for d in range(rows):
        tile = (row + d) % rows * e_rows // TILE
        keep = lax.dynamic_index_in_dim(kept, tile, 1, keepdims=True) > 0
        best.append(jnp.where(keep, back[d][:n], floor_value))
        soft.append(jnp.where(keep, back[d][n:], 0.0))
    return jnp.max(jnp.stack(best), axis=(0, 1)), jnp.log1p(jnp.sum(jnp.stack(soft), axis=(0, 1)))


def solution(mesh):
    in_specs = (P(("row", "col"), None), P(("col", "row"), None), P("row", "col"))
    out_specs = (P(("row", "col")), P(("row", "col")))
    return jax.shard_map(
        on_device, mesh=mesh, in_specs=in_specs, out_specs=out_specs, check_vma=False
    )
```
